512 devices in a mesh: dp: 4 (over x), fsdp: 4 (over y_hi, core), tensor: 32 (over z, y_lo).
Axes of the slice: x: 4, y: 4 (y_hi: 2, y_lo: 2; y = y_hi * 2 + y_lo), z: 16, core: 2. Of those that a mesh axis runs over, the one named last changes fastest.
Arguments:
- activations: bfloat16 [4096, 4096], P(('dp', 'tensor'), 'fsdp'), may hold values from -6 to 6
- cotangent: bfloat16 [4096, 16384], P('dp', 'tensor'), may hold values from -6 to 6
- weight: bfloat16 [4096, 16384], P('fsdp', 'tensor'), may hold values from -0.046875 to 0.046875
- residual: bfloat16 [4, 4096, 16384], P('dp', 'fsdp', 'tensor'), may hold values from -6 to 6
- step_size: float32 [1], replicated, may hold values from 0.02 to 0.06
- kept_blocks: int32 [4, 4, 32, 8], P('dp', 'fsdp', 'tensor'), may hold values from 0 to 31, as said below
Outputs:
- input_grad: bfloat16 [4096, 4096], P(('dp', 'tensor'), 'fsdp')
- residual_out: bfloat16 [4, 4096, 16384], P('dp', 'fsdp', 'tensor')
- owned: float32 [4, 4, 32, 8, 128, 128], P('dp', 'fsdp', 'tensor')
The draws below stay inside these ranges and needn't reach their ends.
Inputs may be any that keep to these rules, and one draw needn't show every extreme that they name: The 8 entries of kept_blocks[a, f, t, :] are different block numbers.
All inputs are finite; a program needn't handle non-finite values.
Results may differ from the reference program's by a relative error of at most 0.0029.
Values may be sent and summed in bfloat16 or wider, within the bound.
A program may use at most 64 MiB of HBM per device.

```python
import math
import jax
import jax.numpy as jnp
from jax import lax

D = 4096
FW = 16384
BLK = 128
KEEP = 8
TOKG = 1024
TOK = 4096
REGION_BLOCKS = 32
N_DP = 4
N_FSDP = 4
N_TENSOR = 32


def draw_kept_blocks(key, part):
    first_key, second_key = jax.random.split(jax.random.fold_in(key, 7))
    preferred_blocks = jax.random.randint(first_key, (1, N_FSDP, N_TENSOR, 1), 0, N_DP)
    baseline_score = jax.random.randint(second_key, (N_DP, N_FSDP, N_TENSOR, REGION_BLOCKS), 0, 1 << 16)
    block_numbers = jnp.arange(REGION_BLOCKS, dtype=jnp.int32)
    extra_credit = jnp.where((block_numbers % N_DP)[None, None, None, :] == preferred_blocks, 1 << 15, 0)
    block_scores = (baseline_score + extra_credit) * REGION_BLOCKS + block_numbers[None, None, None, :]
    chosen = lax.top_k(block_scores, KEEP)[1]
    return chosen.astype(jnp.int32)


def raised(result, rng, source, target, parts, factor):
    def block_of(axis_at):
        return (jnp.arange(result.shape[axis_at]) // (result.shape[axis_at] // parts)).reshape((-1,) + (1,) * (result.ndim - 1 - axis_at))

    one_side = jax.random.permutation(rng, parts)[block_of(target)]
    far = (block_of(target) + parts // 2) % parts
    return jnp.where((block_of(source) == one_side) | (block_of(source) == far), factor * result, result)


def levels(rng, extent, cuts, least, largest):
    level, own = 1.0, jax.random.fold_in(rng, 6)
    for dim, shards_of in cuts:
        draws = jnp.exp(jax.random.uniform(jax.random.fold_in(own, dim), (shards_of,), jnp.float32, least / len(cuts), largest / len(cuts)))
        level = level * jnp.repeat(draws, extent[dim] // shards_of).reshape([-1 if axis == dim else 1 for axis in range(len(extent))])
    return level


def centred(stream_key, shape, deviation, reach, cuts=(), kind=jnp.bfloat16):
    drawn = jax.random.normal(stream_key, shape, jnp.float32) * deviation
    if len(cuts) > 0:
        drawn = levels(stream_key, shape, cuts, -0.22, 0.18) * drawn
    return jnp.clip(drawn, min=-reach, max=reach).astype(kind)


def noise_with(rng, dims, scale, reach, cuts, heavy, kind=jnp.bfloat16):
    entries = scale * jax.random.normal(rng, dims, jnp.float32)
    if cuts:
        entries = entries * levels(rng, dims, cuts, -0.22, 0.18)
    return jnp.clip(raised(entries, jax.random.fold_in(rng, 3), *heavy), -reach, reach).astype(kind)


def setup_inputs(seed: int = 0) -> dict:
    key_of = jax.random.split(jax.random.key(seed), 7)
    return {
        "activations": centred(key_of[0], (TOK, D), 1.0, 6.0, ((0, 128), (1, 4))),
        "cotangent": noise_with(key_of[1], (TOK, FW), 1.0, 6.0, ((0, 4), (1, 32)), (1, 0, 32, 2.75)),
        "weight": centred(key_of[2], (D, FW), FW ** -0.5, 0.046875, ((0, 4), (1, 32))),
        "residual": centred(key_of[3], (N_DP, D, FW), 1.0, 6.0, ((0, 4), (1, 4), (2, 32))),
        "step_size": jnp.clip(jnp.exp(jax.random.uniform(key_of[4], (1,), jnp.float32, math.log(0.02), math.log(0.06))), 0.02, 0.06),
        "kept_blocks": draw_kept_blocks(jax.random.fold_in(key_of[6], 71), 0),
    }


def reference(activations, cotangent, weight, residual, step_size, kept_blocks):
    row_block_count = D // (BLK * N_FSDP)
    col_blocks = FW // (BLK * N_TENSOR)
    count = row_block_count * col_blocks
    block_numbers = jnp.arange(count, dtype=jnp.int32)
    zero = jnp.zeros((), jnp.bfloat16)

    def one_group(total, inputs):
        acts, cots, resid, picks = inputs
        gradient = jnp.dot(acts.T, cots, preferred_element_type=jnp.float32)
        accumulated = resid.astype(jnp.float32) + step_size[0] * gradient
        rounded = accumulated.astype(jnp.bfloat16)
        chosen = jnp.any(block_numbers[None, None, :, None] == picks[:, :, None, :], axis=3)
        chosen = chosen.reshape(N_FSDP, N_TENSOR, row_block_count, col_blocks).transpose(0, 2, 1, 3)
        chosen = chosen[:, :, None, :, :, None]
        shaped = rounded.reshape(N_FSDP, row_block_count, BLK, N_TENSOR, col_blocks, BLK)
        sent = jnp.where(chosen, shaped, zero)
        new_resid = jnp.where(chosen, zero, shaped).reshape(D, FW)
        blocks = sent.transpose(0, 3, 1, 4, 2, 5).reshape(N_FSDP, N_TENSOR, count, BLK, BLK)
        return total + blocks.astype(jnp.float32), new_resid

    initial_total = jnp.zeros((N_FSDP, N_TENSOR, count, BLK, BLK), jnp.float32)
    inputs = (activations.reshape(N_DP, TOKG, D), cotangent.reshape(N_DP, TOKG, FW), residual, kept_blocks)
    total, residual_out = lax.scan(one_group, initial_total, inputs)
    owned = total.reshape(N_FSDP, N_TENSOR, count // N_DP, N_DP, BLK, BLK).transpose(3, 0, 1, 2, 4, 5)

    input_grad = jnp.dot(cotangent, weight.T, preferred_element_type=jnp.float32).astype(jnp.bfloat16)
    return input_grad, residual_out, owned
```

```python
import functools

import jax
import jax.numpy as jnp
from jax import lax
from jax.experimental import pallas as pl
from jax.experimental.pallas import tpu as pltpu
from jax.sharding import PartitionSpec as P

BLK = 128
MESH = pl.DeviceIdType.MESH
NT = (((1,), (1,)), ((), ()))
F32 = jnp.float32
BF16 = jnp.bfloat16


def kernel(
    step_ref, kept_ref, acts_ref, cot_hbm, w_hbm, res_hbm,
    ig_ref, ro_ref, ow_ref,
    full, cot, w, res, own, yout, yin, ring, sent, dpin,
    local_sem, pair_send, pair_recv, ag_send, ag_recv, ya_send, ya_recv,
    yr_send, yr_recv, rs_send, rs_recv, dp_send, dp_recv,
):
    planes = cot.shape[0]
    half = planes // 2
    rows = cot.shape[2]
    hid = cot.shape[3]
    cols = full.shape[4]
    a = lax.axis_index("dp")
    f = lax.axis_index("fsdp")
    t = lax.axis_index("tensor")
    groups = lax.axis_size("dp")
    z = t // 2
    par = t % 2

    def plane(p):
        return lax.rem(p + 2 * planes, planes)

    up = (a, f, plane(z + 1) * 2 + par)
    down = (a, f, plane(z - 1) * 2 + par)
    pair = (a, f, z * 2 + 1 - par)
    zdev = (up, down)
    sign = (1, -1)

    def dpdev(k):
        return (lax.rem(a + k, groups), f, t)

    def remote(src, dst, send, recv, dev):
        return pltpu.make_async_remote_copy(
            src_ref=src, dst_ref=dst, send_sem=send, recv_sem=recv, device_id=dev, device_id_type=MESH
        )

    loads = [
        pltpu.make_async_copy(acts_ref.at[:, pl.ds(0, cols)], full.at[0, z, par], local_sem.at[0]),
        pltpu.make_async_copy(acts_ref.at[:, pl.ds(cols, cols)], full.at[1, z, par], local_sem.at[1]),
        pltpu.make_async_copy(cot_hbm, cot, local_sem.at[2]),
        pltpu.make_async_copy(w_hbm, w, local_sem.at[3]),
        pltpu.make_async_copy(res_hbm, res, local_sem.at[4]),
    ]
    for load in loads:
        load.start()

    barrier = pltpu.get_barrier_semaphore()
    others = [up, down, pair] + [dpdev(k) for k in range(1, groups)]
    for dev in others:
        pl.semaphore_signal(barrier, inc=1, device_id=dev, device_id_type=MESH)
    pl.semaphore_wait(barrier, len(others))

    def pair_copy():
        return remote(full.at[0, z, par], full.at[0, z, par], pair_send, pair_recv, pair)

    def pair_arrival():
        return remote(full.at[0, z, 1 - par], full.at[0, z, 1 - par], pair_send, pair_recv, pair)

    def gather_copy(h, d, s):
        p = plane(z - sign[d] * s)
        if h == 0:
            ref = full.at[0, p]
        else:
            ref = full.at[1, p, par]
        return remote(ref, ref, ag_send.at[h, d, s], ag_recv.at[h, d, s], zdev[d])

    def gather_arrival(h, d, s):
        p = plane(z - sign[d] * (s + 1))
        if h == 0:
            ref = full.at[0, p]
        else:
            ref = full.at[1, p, par]
        return remote(ref, ref, ag_send.at[h, d, s], ag_recv.at[h, d, s], zdev[d])

    def across_copy(p):
        ref = full.at[1, p, par]
        return remote(ref, ref, ya_send.at[p], ya_recv.at[p], pair)

    def across_arrival(p):
        ref = full.at[1, p, 1 - par]
        return remote(ref, ref, ya_send.at[p], ya_recv.at[p], pair)

    def exchange_plane(q):
        i = (q + 1) // 2
        return plane(z + (2 * (q % 2) - 1) * (half - i))

    def exchange_copy(p):
        return remote(yout.at[p], yin.at[p], yr_send.at[p], yr_recv.at[p], pair)

    def ring_copy(d, h, k, p):
        return remote(
            own.at[p, h], ring.at[d, h, k - 1], rs_send.at[d, h, k], rs_recv.at[d, h, k - 1], zdev[d]
        )

    def ring_arrival(d, h, k, p):
        return remote(
            own.at[p, h], ring.at[d, h, k], rs_send.at[d, h, k], rs_recv.at[d, h, k], zdev[d]
        )

    def dp_copy(k, g):
        lines = pl.ds(pl.multiple_of(g * 2 * BLK, 2 * BLK), 2 * BLK)
        return remote(
            sent.at[lax.rem(a + k, groups), lines], dpin.at[k - 1, lines],
            dp_send.at[k - 1, g], dp_recv.at[k - 1, g], dpdev(k),
        )

    def hops(h, d):
        return half if h == d else half - 1

    loads[0].wait()
    loads[1].wait()
    pair_copy().start()
    gather_copy(1, 0, 0).start()
    gather_copy(1, 1, 0).start()
    across_copy(z).start()
    loads[2].wait()
    loads[3].wait()

    def partial(b, parity):
        x = cot[pl.ds(b * half, half), parity].reshape(half * rows, hid)
        return lax.dot_general(x, w[...], NT, preferred_element_type=F32).reshape(half, rows, 2 * cols)

    def theirs(b, carry):
        y = partial(b, 1 - par).astype(BF16)
        yout[pl.ds(b * half, half), 0] = y[:, :, :cols]
        yout[pl.ds(b * half, half), 1] = y[:, :, cols:]
        return carry

    def ours(b, carry):
        y = partial(b, par)
        own[pl.ds(b * half, half), 0] = y[:, :, :cols]
        own[pl.ds(b * half, half), 1] = y[:, :, cols:]
        return carry

    theirs(0, 0)
    pair_arrival().wait_recv()
    gather_copy(0, 0, 0).start()
    gather_copy(0, 1, 0).start()
    theirs(1, 0)
    for q in range(2):
        exchange_copy(exchange_plane(q)).start()
    lax.fori_loop(0, 2, ours, 0)

    def gather_step(s, carry):
        for h in (1, 0):
            for d in range(2):
                gather_arrival(h, d, s).wait_recv()
                if h == d:
                    gather_copy(h, d, s + 1).start()
                else:
                    @pl.when(s + 1 < half - 1)
                    def _():
                        gather_copy(h, d, s + 1).start()
                if h == 1:
                    across_copy(plane(z - sign[d] * (s + 1))).start()
        exchange_copy(exchange_plane(s + 2)).start()
        return carry

    lax.fori_loop(0, half - 1, gather_step, 0)
    gather_arrival(1, 1, half - 1).wait_recv()
    across_copy(plane(z + half)).start()
    gather_arrival(0, 0, half - 1).wait_recv()

    def rest(q, carry):
        exchange_copy(exchange_plane(q)).start()
        return carry

    lax.fori_loop(half + 1, planes, rest, 0)

    def exchanged(p):
        remote(yout.at[p], yin.at[p], yr_send.at[p], yr_recv.at[p], pair).wait_recv()

    far = plane(z + half)
    exchanged(far)
    for d in range(2):
        own[far, d] = own[far, d] + yin[far, d].astype(F32)
        ring_copy(d, d, half, far).start()

    def ring_step(k, first):
        for d in range(2):
            p = plane(z + sign[d] * k)
            exchanged(p)
            for h in (d, 1 - d):
                total = own[p, h] + yin[p, h].astype(F32)
                if not (first and h != d):
                    ring_arrival(d, h, k, p).wait_recv()
                    total = total + ring[d, h, k]
                own[p, h] = total
                ring_copy(d, h, k, p).start()

    step = step_ref[0]
    kept = [kept_ref[i] for i in range(kept_ref.shape[0])]

    def gradient(g):
        h = g // 2
        lanes = pl.ds(pl.multiple_of((g % 2) * 2 * BLK, 2 * BLK), 2 * BLK)
        lines = pl.ds(pl.multiple_of(g * 2 * BLK, 2 * BLK), 2 * BLK)
        x = full[h, :, :, :, lanes].reshape(planes * 2 * rows, 2 * BLK)
        y = cot[...].reshape(planes * 2 * rows, hid)
        grad = lax.dot_general(x, y, (((0,), (0,)), ((), ())), preferred_element_type=F32)
        rounded = (res[lines].astype(F32) + step * grad).astype(BF16)
        for i in range(2):
            for o in range(groups):
                number = (2 * g + i) * groups + o
                hit = kept[0] == number
                for other in kept[1:]:
                    hit = jnp.logical_or(hit, other == number)
                keep = jnp.where(hit, 1.0, 0.0)
                block = rounded[i * BLK:(i + 1) * BLK, o * BLK:(o + 1) * BLK].astype(F32)
                here = pl.ds(pl.multiple_of((2 * g + i) * BLK, BLK), BLK)
                ro_ref[here, o * BLK:(o + 1) * BLK] = (block * (1.0 - keep)).astype(BF16)
                sent[o, here] = (block * keep).astype(BF16)
        for k in range(1, groups):
            dp_copy(k, g).start()

    ring_step(half - 1, True)
    lax.fori_loop(0, planes, lambda p, c: (across_arrival(p).wait_recv(), c)[1], 0)
    loads[4].wait()

    def both(s, carry):
        ring_step(half - 1 - s, False)

        @pl.when(s <= groups)
        def _():
            gradient(s - 1)

        return carry

    lax.fori_loop(1, half - 1, both, 0)

    exchanged(z)
    for h in range(2):
        total = own[z, h] + yin[z, h].astype(F32)
        for d in range(2):
            ring_arrival(d, h, 0, z).wait_recv()
            total = total + ring[d, h, 0]
        ig_ref[:, h * cols:(h + 1) * cols] = total.astype(BF16)

    total = sent[a].astype(F32)
    for k in range(1, groups):
        for g in range(4):
            dp_copy(k, g).wait_recv()
        total = total + dpin[k - 1].astype(F32)
    ow_ref[...] = total

    pair_copy().wait_send()
    for h in range(2):
        for d in range(2):
            lax.fori_loop(0, hops(h, d), lambda s, c: (gather_copy(h, d, s).wait_send(), c)[1], 0)
            lax.fori_loop(
                1, hops(h, d) + 1,
                lambda k, c: (ring_copy(d, h, k, plane(z + sign[d] * k)).wait_send(), c)[1], 0,
            )

    def drain(p, carry):
        across_copy(p).wait_send()
        exchange_copy(p).wait_send()
        return carry

    lax.fori_loop(0, planes, drain, 0)
    for k in range(1, groups):
        for g in range(4):
            dp_copy(k, g).wait_send()


def body(activations, cotangent, weight, residual, step_size, kept_blocks):
    rows, width = activations.shape
    hid = cotangent.shape[1]
    pairs = cotangent.shape[0] // (2 * rows)
    half = pairs // 2
    cols = width // 2
    groups = lax.axis_size("dp")
    vmem = pl.BlockSpec(memory_space=pltpu.VMEM)
    smem = pl.BlockSpec(memory_space=pltpu.SMEM)
    hbm = pl.BlockSpec(memory_space=pl.ANY)
    dma = pltpu.SemaphoreType.DMA
    input_grad, residual_out, owned = pl.pallas_call(
        kernel,
        out_shape=(
            jax.ShapeDtypeStruct((rows, width), BF16),
            jax.ShapeDtypeStruct((width, hid), BF16),
            jax.ShapeDtypeStruct((width, BLK), F32),
        ),
        in_specs=[smem, smem, hbm, hbm, hbm, hbm],
        out_specs=(vmem, vmem, vmem),
        scratch_shapes=[
            pltpu.VMEM((2, pairs, 2, rows, cols), BF16),
            pltpu.VMEM((pairs, 2, rows, hid), BF16),
            pltpu.VMEM((width, hid), BF16),
            pltpu.VMEM((width, hid), BF16),
            pltpu.VMEM((pairs, 2, rows, cols), F32),
            pltpu.VMEM((pairs, 2, rows, cols), BF16),
            pltpu.VMEM((pairs, 2, rows, cols), BF16),
            pltpu.VMEM((2, 2, half, rows, cols), F32),
            pltpu.VMEM((groups, width, BLK), BF16),
            pltpu.VMEM((groups - 1, width, BLK), BF16),
            dma((5,)),
            dma, dma,
            dma((2, 2, half)), dma((2, 2, half)),
            dma((pairs,)), dma((pairs,)),
            dma((pairs,)), dma((pairs,)),
            dma((2, 2, half + 1)), dma((2, 2, half + 1)),
            dma((groups - 1, 4)), dma((groups - 1, 4)),
        ],
        compiler_params=pltpu.CompilerParams(
            collective_id=0, has_side_effects=True, vmem_limit_bytes=60 * 1024 * 1024
        ),
    )(
        step_size,
        kept_blocks.reshape(-1),
        activations,
        cotangent.reshape(pairs, 2, rows, hid),
        weight,
        residual[0],
    )
    return (
        input_grad,
        residual_out[None],
        owned.reshape(1, 1, 1, width // BLK, BLK, BLK),
    )


def solution(mesh):
    return jax.shard_map(
        body,
        mesh=mesh,
        in_specs=(
            P(("dp", "tensor"), "fsdp"),
            P("dp", "tensor"),
            P("fsdp", "tensor"),
            P("dp", "fsdp", "tensor"),
            P(),
            P("dp", "fsdp", "tensor", None),
        ),
        out_specs=(
            P(("dp", "tensor"), "fsdp"),
            P("dp", "fsdp", "tensor"),
            P("dp", "fsdp", "tensor", None, None, None),
        ),
        check_vma=False,
    )
```

```python
import contextlib

import jax
import jax.numpy as jnp
from jax import lax
from jax.experimental import pallas as pl
from jax.experimental.pallas import tpu as pltpu
from jax.sharding import PartitionSpec as P

BLK = 128
MESH = pl.DeviceIdType.MESH
NT = (((1,), (1,)), ((), ()))
F32 = jnp.float32
BF16 = jnp.bfloat16
AHEAD = 3
scope = lambda name: contextlib.nullcontext()


def kernel(
    step_ref, kept_hbm, acts_ref, cot_hbm, w_hbm, res_hbm,
    ig_ref, ro_ref, ow_ref,
    full, cot, w, res, own, yout, yin, ring, sent, dpin, kept_ref,
    local_sem, pair_send, pair_recv, ag_send, ag_recv, ya_send, ya_recv,
    yr_send, yr_recv, rs_send, rs_recv, dp_send, dp_recv,
):
    planes = cot.shape[0]
    half = planes // 2
    rows = cot.shape[2]
    part = rows // 2
    hid = cot.shape[3]
    cols = full.shape[4]
    a = lax.axis_index("dp")
    f = lax.axis_index("fsdp")
    t = lax.axis_index("tensor")
    groups = lax.axis_size("dp")
    z = t // 2
    par = t % 2

    def plane(p):
        return lax.rem(p + 2 * planes, planes)

    up = (a, f, plane(z + 1) * 2 + par)
    down = (a, f, plane(z - 1) * 2 + par)
    pair = (a, f, z * 2 + 1 - par)
    zdev = (up, down)
    sign = (1, -1)

    def dpdev(k):
        return (lax.rem(a + k, groups), f, t)

    def remote(src, dst, send, recv, dev):
        return pltpu.make_async_remote_copy(
            src_ref=src, dst_ref=dst, send_sem=send, recv_sem=recv, device_id=dev, device_id_type=MESH
        )

    loads = [
        pltpu.make_async_copy(acts_ref.at[:, pl.ds(0, cols)], full.at[0, z, par], local_sem.at[0]),
        pltpu.make_async_copy(acts_ref.at[:, pl.ds(cols, cols)], full.at[1, z, par], local_sem.at[1]),
        pltpu.make_async_copy(cot_hbm, cot, local_sem.at[2]),
        pltpu.make_async_copy(w_hbm, w, local_sem.at[3]),
        pltpu.make_async_copy(res_hbm, res, local_sem.at[4]),
        pltpu.make_async_copy(kept_hbm, kept_ref, local_sem.at[5]),
    ]
    for load in loads:
        load.start()

    with scope("bar"):
        barrier = pltpu.get_barrier_semaphore()
        others = [up, down, pair] + [dpdev(k) for k in range(1, groups)]
        for dev in others:
            pl.semaphore_signal(barrier, inc=1, device_id=dev, device_id_type=MESH)
        pl.semaphore_wait(barrier, len(others))

    def pair_copy():
        return remote(full.at[0, z, par], full.at[0, z, par], pair_send, pair_recv, pair)

    def pair_arrival():
        return remote(full.at[0, z, 1 - par], full.at[0, z, 1 - par], pair_send, pair_recv, pair)

    chains = ((1, par), (0, par), (0, 1 - par))

    def longer(h, d):
        return lax.rem(h + d, 2)

    def hops(h, d):
        return half if h == d else half - 1

    def gather_copy(c, d, s):
        h, q = chains[c]
        ref = full.at[h, plane(z - sign[d] * s), q]
        return remote(ref, ref, ag_send.at[c, d, s], ag_recv.at[c, d, s], zdev[d])

    def gather_arrival(c, d, s):
        h, q = chains[c]
        ref = full.at[h, plane(z - sign[d] * (s + 1)), q]
        return remote(ref, ref, ag_send.at[c, d, s], ag_recv.at[c, d, s], zdev[d])

    def across_copy(p):
        ref = full.at[1, p, par]
        return remote(ref, ref, ya_send.at[p], ya_recv.at[p], pair)

    def across_arrival(p):
        ref = full.at[1, p, 1 - par]
        return remote(ref, ref, ya_send.at[p], ya_recv.at[p], pair)

    def exchange_copy(p, h):
        return remote(yout.at[p, h], yin.at[p, h], yr_send.at[p, h], yr_recv.at[p, h], pair)

    def ring_copy(d, h, i, k, p):
        lines = pl.ds(i * part, part)
        return remote(
            own.at[p, h, lines], ring.at[d, h, k - 1, lines],
            rs_send.at[d, h, i, k], rs_recv.at[d, h, i, k - 1], zdev[d],
        )

    def ring_arrival(d, h, i, k, p):
        lines = pl.ds(i * part, part)
        return remote(
            own.at[p, h, lines], ring.at[d, h, k, lines],
            rs_send.at[d, h, i, k], rs_recv.at[d, h, i, k], zdev[d],
        )

    def dp_copy(k, g):
        lines = pl.ds(pl.multiple_of(g * 2 * BLK, 2 * BLK), 2 * BLK)
        return remote(
            sent.at[lax.rem(a + k, groups), lines], dpin.at[k - 1, lines],
            dp_send.at[k - 1, g], dp_recv.at[k - 1, g], dpdev(k),
        )

    def partial(b, parity):
        x = cot[pl.ds(b * half, half), parity].reshape(half * rows, hid)
        return lax.dot_general(x, w[...], NT, preferred_element_type=F32).reshape(half, rows, 2 * cols)

    def theirs(b):
        y = partial(b, 1 - par).astype(BF16)
        yout[pl.ds(b * half, half), 0] = y[:, :, :cols]
        yout[pl.ds(b * half, half), 1] = y[:, :, cols:]

    def ours(b):
        y = partial(b, par)
        own[pl.ds(b * half, half), 0] = y[:, :, :cols]
        own[pl.ds(b * half, half), 1] = y[:, :, cols:]

    def gather_step(s):
        for c in range(3):
            for d in range(2):
                h = chains[c][0]

                def arrive():
                    gather_arrival(c, d, s).wait_recv()
                    if h == 1:
                        across_copy(plane(z - sign[d] * (s + 1))).start()

                if h == d:
                    arrive()
                else:
                    pl.when(s + 1 < half)(arrive)

                @pl.when(s + 1 < hops(h, d))
                def _():
                    gather_copy(c, d, s + 1).start()

    def exchange(r):
        h, k = r % 2, half - r // 2
        exchange_copy(plane(z + k), h).start()

        @pl.when((k > 0) & (k < half))
        def _():
            exchange_copy(plane(z - k), h).start()

    def ring_step(r):
        h, k = r % 2, half - r // 2
        for d in range(2):
            p = plane(z + sign[d] * k)

            def ring_part():
                exchange_copy(p, h).wait_recv()
                for i in range(2):
                    lines = pl.ds(i * part, part)

                    @pl.when(k < half - longer(h, d))
                    def _():
                        ring_arrival(d, h, i, k, p).wait_recv()
                        own[p, h, lines] = own[p, h, lines] + ring[d, h, k, lines]

                    own[p, h, lines] = own[p, h, lines] + yin[p, h, lines].astype(F32)
                    ring_copy(d, h, i, k, p).start()

            pl.when(k <= half - longer(h, d))(ring_part)

    def gradient(g):
        h = g // 2
        lanes = pl.ds(pl.multiple_of((g % 2) * 2 * BLK, 2 * BLK), 2 * BLK)
        lines = pl.ds(pl.multiple_of(g * 2 * BLK, 2 * BLK), 2 * BLK)
        step = step_ref[0]
        kept = [kept_ref[i] for i in range(kept_ref.shape[0])]
        x = full[h, :, :, :, lanes].reshape(planes * 2 * rows, 2 * BLK)
        y = cot[...].reshape(planes * 2 * rows, hid)
        grad = lax.dot_general(x, y, (((0,), (0,)), ((), ())), preferred_element_type=F32)
        rounded = (res[lines].astype(F32) + step * grad).astype(BF16)
        for i in range(2):
            for o in range(groups):
                number = (2 * g + i) * groups + o
                hit = kept[0] == number
                for other in kept[1:]:
                    hit = jnp.logical_or(hit, other == number)
                keep = jnp.where(hit, 1.0, 0.0)
                block = rounded[i * BLK:(i + 1) * BLK, o * BLK:(o + 1) * BLK].astype(F32)
                here = pl.ds(pl.multiple_of((2 * g + i) * BLK, BLK), BLK)
                ro_ref[here, o * BLK:(o + 1) * BLK] = (block * (1.0 - keep)).astype(BF16)
                sent[o, here] = (block * keep).astype(BF16)
        for k in range(1, groups):
            dp_copy(k, g).start()

    def loop(first, last, f):
        lax.fori_loop(first, last, lambda i, c: (f(i), c)[1], 0)

    with scope("ld0"):
        loads[0].wait()
        loads[1].wait()
    pair_copy().start()
    for c in range(2):
        for d in range(2):
            gather_copy(c, d, 0).start()
    across_copy(z).start()
    with scope("ld2"):
        loads[2].wait()
        loads[3].wait()
    with scope("theirs"):
        loop(0, 2, theirs)
    with scope("pair"):
        pair_arrival().wait_recv()
        for d in range(2):
            gather_copy(2, d, 0).start()
    loop(0, AHEAD, exchange)
    with scope("ours"):
        loop(0, 2, ours)

    def slot(s):
        @pl.when(s < half)
        def _():
            with scope("ag"):
                gather_step(s)

        @pl.when(s + AHEAD < planes + 2)
        def _():
            exchange(s + AHEAD)

        with scope("rs"):
            ring_step(s)

        @pl.when(s == half - 1)
        def _():
            with scope("across"):
                loop(0, planes, lambda p: across_arrival(p).wait_recv())
                for load in loads[4:]:
                    load.wait()

        @pl.when((s >= half - 1) & (s < half + 3))
        def _():
            with scope("grad"):
                gradient(s - half + 1)

    loop(0, planes, slot)

    with scope("rs_last"):
        for h in range(2):
            exchange_copy(z, h).wait_recv()
            for i in range(2):
                lines = pl.ds(i * part, part)
                total = own[z, h, lines] + yin[z, h, lines].astype(F32)
                for d in range(2):
                    ring_arrival(d, h, i, 0, z).wait_recv()
                    total = total + ring[d, h, 0, lines]
                ig_ref[lines, h * cols:(h + 1) * cols] = total.astype(BF16)

    with scope("dpsum"):
        total = sent[a].astype(F32)
        for k in range(1, groups):
            for g in range(4):
                dp_copy(k, g).wait_recv()
            total = total + dpin[k - 1].astype(F32)
        ow_ref[...] = total

    with scope("drain"):
        pair_copy().wait_send()
        for d in range(2):
            for c in range(3):
                loop(0, hops(chains[c][0], d), lambda s: gather_copy(c, d, s).wait_send())
            for h in range(2):
                for i in range(2):
                    loop(
                        1, hops(h, d) + 1,
                        lambda k: ring_copy(d, h, i, k, plane(z + sign[d] * k)).wait_send(),
                    )

        def left(p):
            across_copy(p).wait_send()
            for h in range(2):
                exchange_copy(p, h).wait_send()

        loop(0, planes, left)
        for k in range(1, groups):
            for g in range(4):
                dp_copy(k, g).wait_send()


def place(ig_in, ro_in, ow_in, ig_out, ro_out, ow_out, sem):
    copies = [
        pltpu.make_async_copy(src, dst, sem.at[i])
        for i, (src, dst) in enumerate(((ro_in, ro_out), (ow_in, ow_out), (ig_in, ig_out)))
    ]
    for copy in copies:
        copy.start()
    for copy in copies:
        copy.wait()


def body(activations, cotangent, weight, residual, step_size, kept_blocks):
    rows, width = activations.shape
    hid = cotangent.shape[1]
    pairs = cotangent.shape[0] // (2 * rows)
    half = pairs // 2
    cols = width // 2
    groups = lax.axis_size("dp")
    vmem = pl.BlockSpec(memory_space=pltpu.VMEM)
    smem = pl.BlockSpec(memory_space=pltpu.SMEM)
    hbm = pl.BlockSpec(memory_space=pltpu.HBM)
    dma = pltpu.SemaphoreType.DMA
    results = pl.pallas_call(
        kernel,
        out_shape=(
            pltpu.VMEM((rows, width), BF16),
            pltpu.VMEM((width, hid), BF16),
            pltpu.VMEM((width, BLK), F32),
        ),
        in_specs=[smem] + [hbm] * 5,
        out_specs=(vmem, vmem, vmem),
        scratch_shapes=[
            pltpu.VMEM((2, pairs, 2, rows, cols), BF16),
            pltpu.VMEM((pairs, 2, rows, hid), BF16),
            pltpu.VMEM((width, hid), BF16),
            pltpu.VMEM((width, hid), BF16),
            pltpu.VMEM((pairs, 2, rows, cols), F32),
            pltpu.VMEM((pairs, 2, rows, cols), BF16),
            pltpu.VMEM((pairs, 2, rows, cols), BF16),
            pltpu.VMEM((2, 2, half, rows, cols), F32),
            pltpu.VMEM((groups, width, BLK), BF16),
            pltpu.VMEM((groups - 1, width, BLK), BF16),
            pltpu.SMEM(kept_blocks.shape[-1:], jnp.int32),
            dma((6,)),
            dma, dma,
            dma((3, 2, half)), dma((3, 2, half)),
            dma((pairs,)), dma((pairs,)),
            dma((pairs, 2)), dma((pairs, 2)),
            dma((2, 2, 2, half + 1)), dma((2, 2, 2, half + 1)),
            dma((groups - 1, 4)), dma((groups - 1, 4)),
        ],
        compiler_params=pltpu.CompilerParams(
            collective_id=0, has_side_effects=True, vmem_limit_bytes=48 * 1024 * 1024
        ),
    )(
        step_size,
        *[pltpu.with_memory_space_constraint(x, pltpu.HBM) for x in (
            kept_blocks.reshape(-1),
            activations,
            cotangent.reshape(pairs, 2, rows, hid),
            weight,
            residual[0],
        )]
    )
    input_grad, residual_out, owned = pl.pallas_call(
        place,
        out_shape=tuple(jax.ShapeDtypeStruct(x.shape, x.dtype) for x in results),
        in_specs=[vmem] * 3,
        out_specs=(hbm, hbm, hbm),
        scratch_shapes=[dma((3,))],
    )(*[pltpu.with_memory_space_constraint(x, pltpu.VMEM) for x in results])
    return (
        input_grad,
        residual_out[None],
        owned.reshape(1, 1, 1, width // BLK, BLK, BLK),
    )


def solution(mesh):
    return jax.shard_map(
        body,
        mesh=mesh,
        in_specs=(
            P(("dp", "tensor"), "fsdp"),
            P("dp", "tensor"),
            P("fsdp", "tensor"),
            P("dp", "fsdp", "tensor"),
            P(),
            P("dp", "fsdp", "tensor", None),
        ),
        out_specs=(
            P(("dp", "tensor"), "fsdp"),
            P("dp", "fsdp", "tensor"),
            P("dp", "fsdp", "tensor", None, None, None),
        ),
        check_vma=False,
    )
```

```python
import contextlib

import jax
import jax.numpy as jnp
from jax import lax
from jax.experimental import pallas as pl
from jax.experimental.pallas import tpu as pltpu
from jax.sharding import PartitionSpec as P

BLK = 128
MESH = pl.DeviceIdType.MESH
NT = (((1,), (1,)), ((), ()))
F32 = jnp.float32
BF16 = jnp.bfloat16
scope = lambda name: contextlib.nullcontext()


def kernel(
    step_ref, kept_hbm, acts_ref, cot_hbm, w_hbm, res_hbm,
    ig_ref, ro_ref, ow_ref,
    full, cot, w, res, own, yout, yin, early, ring16, ring, sent, dpin, kept_ref,
    local_sem, pair_send, pair_recv, ag_send, ag_recv, ya_send, ya_recv,
    yr_send, yr_recv, re_send, re_recv, rs_send, rs_recv, dp_send, dp_recv,
):
    planes = cot.shape[0]
    half = planes // 2
    rows = cot.shape[2]
    part = rows // 2
    hid = cot.shape[3]
    cols = full.shape[4]
    a = lax.axis_index("dp")
    f = lax.axis_index("fsdp")
    t = lax.axis_index("tensor")
    groups = lax.axis_size("dp")
    z = t // 2
    par = t % 2

    def plane(p):
        return lax.rem(p + 2 * planes, planes)

    pair = (a, f, z * 2 + 1 - par)
    sign = (1, -1)
    zdev = [(a, f, plane(z + v) * 2 + par) for v in sign]
    zpair = [(a, f, plane(z + v) * 2 + 1 - par) for v in sign]

    def dpdev(k):
        return (lax.rem(a + k, groups), f, t)

    def remote(src, dst, send, recv, dev):
        return pltpu.make_async_remote_copy(
            src_ref=src, dst_ref=dst, send_sem=send, recv_sem=recv, device_id=dev, device_id_type=MESH
        )

    def take(ref, sem):
        pltpu.make_async_copy(ref, ref, sem).wait()

    def loop(first, last, f):
        lax.fori_loop(first, last, lambda i, c: (f(i), c)[1], 0)

    loads = [
        pltpu.make_async_copy(acts_ref.at[:, pl.ds(0, cols)], full.at[0, z, par], local_sem.at[0]),
        pltpu.make_async_copy(acts_ref.at[:, pl.ds(cols, cols)], full.at[1, z, par], local_sem.at[1]),
        pltpu.make_async_copy(cot_hbm, cot, local_sem.at[2]),
        pltpu.make_async_copy(w_hbm, w, local_sem.at[3]),
        pltpu.make_async_copy(res_hbm, res, local_sem.at[4]),
        pltpu.make_async_copy(kept_hbm, kept_ref, local_sem.at[5]),
    ]
    for load in loads:
        load.start()

    with scope("bar"):
        barrier = pltpu.get_barrier_semaphore()
        others = zdev + zpair + [pair] + [dpdev(k) for k in range(1, groups)]
        for dev in others:
            pl.semaphore_signal(barrier, inc=1, device_id=dev, device_id_type=MESH)
        pl.semaphore_wait(barrier, len(others))

    chains = ((1, par), (0, par), (0, 1 - par))

    def shorter(h, d):
        return lax.rem(h + d, 2)

    def hops(h, d):
        return half if h == d else half - 1

    def gather_copy(c, d, s):
        h, q = chains[c]
        ref = full.at[h, plane(z - sign[d] * s), q]
        return remote(ref, ref, ag_send.at[c], ag_recv.at[c, d, s], zdev[d])

    def gather_first(c, d):
        h = chains[c][0]
        ref = full.at[h, z, par]
        return remote(ref, ref, ag_send.at[c], ag_recv.at[c, d, 0], zpair[d] if c == 2 else zdev[d])

    def gather_arrival(c, d, s):
        h, q = chains[c]
        take(full.at[h, plane(z - sign[d] * (s + 1)), q], ag_recv.at[c, d, s])

    def across_copy(p):
        ref = full.at[1, p, par]
        return remote(ref, ref, ya_send, ya_recv, pair)

    def gather_step(s):
        for c in range(3):
            for d in range(2):
                h = chains[c][0]

                def arrive():
                    gather_arrival(c, d, s)
                    if h == 1:
                        across_copy(plane(z - sign[d] * (s + 1))).start()

                if h == d:
                    arrive()
                else:
                    pl.when(s + 1 < half)(arrive)

                @pl.when(s + 1 < hops(h, d))
                def _():
                    gather_copy(c, d, s + 1).start()

    def exchange(r):
        h, k = r % 2, half - r // 2

        def send(p):
            remote(yout.at[p, h], yin.at[p, h], yr_send, yr_recv.at[h, k], pair).start()

        send(plane(z + k))

        @pl.when((k > 0) & (k < half))
        def _():
            send(plane(z - k))

    def exchanged(h, k, n):
        take(yin.at[pl.ds(0, n), 0], yr_recv.at[h, k])

    def early_step(s):
        for h in range(2):
            @pl.when(s == 0)
            def _():
                exchanged(h, half, 1)

            @pl.when(s == 1)
            def _():
                exchanged(h, half - 1, 2)

            for d in range(2):
                p = plane(z + sign[d] * (half - s))

                def pass_on():
                    total = own[p, h] + yin[p, h].astype(F32)
                    early[d, h, s] = total.astype(BF16)
                    remote(
                        early.at[d, h, s], ring16.at[d, h, s],
                        re_send, re_recv.at[d, h, s], zdev[d],
                    ).start()

                if h == d:
                    @pl.when(s == 1)
                    def _():
                        take(ring16.at[d, h, 0], re_recv.at[d, h, 0])
                        own[p, h] = own[p, h] + ring16[d, h, 0].astype(F32)

                    pass_on()
                else:
                    pl.when(s == 1)(pass_on)

    def ring_step(r):
        h, k = r % 2, half - r // 2
        exchanged(h, k, 2)
        for d in range(2):
            p = plane(z + sign[d] * k)

            @pl.when(k == half - 2)
            def _():
                take(ring16.at[d, h, 1], re_recv.at[d, h, 1])
                own[p, h] = own[p, h] + ring16[d, h, 1].astype(F32)

            for i in range(2):
                lines = pl.ds(i * part, part)

                @pl.when(k < half - 2)
                def _():
                    take(ring.at[d, h, k, lines], rs_recv.at[d, h, k, i])
                    own[p, h, lines] = own[p, h, lines] + ring[d, h, k, lines]

                own[p, h, lines] = own[p, h, lines] + yin[p, h, lines].astype(F32)
                remote(
                    own.at[p, h, lines], ring.at[d, h, k - 1, lines],
                    rs_send, rs_recv.at[d, h, k - 1, i], zdev[d],
                ).start()

    def partial(b, parity):
        x = cot[pl.ds(b * half, half), parity].reshape(half * rows, hid)
        return lax.dot_general(x, w[...], NT, preferred_element_type=F32).reshape(half, rows, 2 * cols)

    def theirs(b):
        y = partial(b, 1 - par).astype(BF16)
        yout[pl.ds(b * half, half), 0] = y[:, :, :cols]
        yout[pl.ds(b * half, half), 1] = y[:, :, cols:]

    def ours(b):
        y = partial(b, par)
        own[pl.ds(b * half, half), 0] = y[:, :, :cols]
        own[pl.ds(b * half, half), 1] = y[:, :, cols:]

    def gradient(g):
        h = g // 2
        lanes = pl.ds(pl.multiple_of((g % 2) * 2 * BLK, 2 * BLK), 2 * BLK)
        lines = pl.ds(pl.multiple_of(g * 2 * BLK, 2 * BLK), 2 * BLK)
        step = step_ref[0]
        kept = [kept_ref[i] for i in range(kept_ref.shape[0])]
        x = full[h, :, :, :, lanes].reshape(planes * 2 * rows, 2 * BLK)
        y = cot[...].reshape(planes * 2 * rows, hid)
        grad = lax.dot_general(x, y, (((0,), (0,)), ((), ())), preferred_element_type=F32)
        rounded = (res[lines].astype(F32) + step * grad).astype(BF16)
        for i in range(2):
            for o in range(groups):
                number = (2 * g + i) * groups + o
                hit = kept[0] == number
                for other in kept[1:]:
                    hit = jnp.logical_or(hit, other == number)
                keep = jnp.where(hit, 1.0, 0.0)
                block = rounded[i * BLK:(i + 1) * BLK, o * BLK:(o + 1) * BLK].astype(F32)
                here = pl.ds(pl.multiple_of((2 * g + i) * BLK, BLK), BLK)
                ro_ref[here, o * BLK:(o + 1) * BLK] = (block * (1.0 - keep)).astype(BF16)
                sent[o, here] = (block * keep).astype(BF16)
        for k in range(1, groups):
            remote(
                sent.at[lax.rem(a + k, groups), lines], dpin.at[k - 1, lines], dp_send, dp_recv, dpdev(k)
            ).start()

    with scope("ld0"):
        loads[0].wait()
        loads[1].wait()
    for c in range(3):
        for d in range(2):
            gather_first(c, d).start()
    pair_copy = remote(full.at[0, z, par], full.at[0, z, par], pair_send, pair_recv, pair)
    pair_copy.start()
    across_copy(z).start()
    with scope("ld2"):
        loads[2].wait()
        loads[3].wait()
    with scope("theirs"):
        loop(0, 2, theirs)
    loop(0, 4, exchange)
    with scope("ours"):
        loop(0, 2, ours)

    def slot(s):
        @pl.when(s < half)
        def _():
            with scope("ag"):
                gather_step(s)

        @pl.when(s + 4 < planes + 2)
        def _():
            exchange(s + 4)

        @pl.when(s < 2)
        def _():
            with scope("early"):
                early_step(s)

        @pl.when(s >= 2)
        def _():
            with scope("rs"):
                ring_step(s + 2)

        @pl.when(s == half - 1)
        def _():
            take(full.at[0, z, 1 - par], pair_recv)
            for load in loads[4:]:
                load.wait()

        @pl.when(s == half + 1)
        def _():
            with scope("across"):
                take(full.at[1, :, 1 - par], ya_recv)

        @pl.when((s >= half - 1) & (s < half + 3))
        def _():
            with scope("grad"):
                gradient(s - half + 1)

    loop(0, planes - 2, slot)

    with scope("rs_last"):
        for h in range(2):
            exchanged(h, 0, 1)
            for i in range(2):
                lines = pl.ds(i * part, part)
                total = own[z, h, lines] + yin[z, h, lines].astype(F32)
                for d in range(2):
                    take(ring.at[d, h, 0, lines], rs_recv.at[d, h, 0, i])
                    total = total + ring[d, h, 0, lines]
                ig_ref[lines, h * cols:(h + 1) * cols] = total.astype(BF16)

    with scope("dpsum"):
        take(dpin, dp_recv)
        total = sent[a].astype(F32)
        for k in range(1, groups):
            total = total + dpin[k - 1].astype(F32)
        ow_ref[...] = total

    with scope("drain"):
        pair_copy.wait_send()
        for c in range(3):
            take(full.at[0, pl.ds(0, planes - 1), 0], ag_send.at[c])
        take(full.at[0, :, 0], ya_send)
        take(yout, yr_send)
        take(yout.at[pl.ds(0, 3)], re_send)
        take(own.at[pl.ds(0, 2 * (half - 2))], rs_send)
        take(dpin, dp_send)


def place(ig_in, ro_in, ow_in, ig_out, ro_out, ow_out, sem):
    copies = [
        pltpu.make_async_copy(src, dst, sem.at[i])
        for i, (src, dst) in enumerate(((ro_in, ro_out), (ow_in, ow_out), (ig_in, ig_out)))
    ]
    for copy in copies:
        copy.start()
    for copy in copies:
        copy.wait()


def body(activations, cotangent, weight, residual, step_size, kept_blocks):
    rows, width = activations.shape
    hid = cotangent.shape[1]
    pairs = cotangent.shape[0] // (2 * rows)
    half = pairs // 2
    cols = width // 2
    groups = lax.axis_size("dp")
    vmem = pl.BlockSpec(memory_space=pltpu.VMEM)
    smem = pl.BlockSpec(memory_space=pltpu.SMEM)
    hbm = pl.BlockSpec(memory_space=pltpu.HBM)
    dma = pltpu.SemaphoreType.DMA
    results = pl.pallas_call(
        kernel,
        out_shape=(
            pltpu.VMEM((rows, width), BF16),
            pltpu.VMEM((width, hid), BF16),
            pltpu.VMEM((width, BLK), F32),
        ),
        in_specs=[smem] + [hbm] * 5,
        out_specs=(vmem, vmem, vmem),
        scratch_shapes=[
            pltpu.VMEM((2, pairs, 2, rows, cols), BF16),
            pltpu.VMEM((pairs, 2, rows, hid), BF16),
            pltpu.VMEM((width, hid), BF16),
            pltpu.VMEM((width, hid), BF16),
            pltpu.VMEM((pairs, 2, rows, cols), F32),
            pltpu.VMEM((pairs, 2, rows, cols), BF16),
            pltpu.VMEM((pairs, 2, rows, cols), BF16),
            pltpu.VMEM((2, 2, 2, rows, cols), BF16),
            pltpu.VMEM((2, 2, 2, rows, cols), BF16),
            pltpu.VMEM((2, 2, half - 2, rows, cols), F32),
            pltpu.VMEM((groups, width, BLK), BF16),
            pltpu.VMEM((groups - 1, width, BLK), BF16),
            pltpu.SMEM(kept_blocks.shape[-1:], jnp.int32),
            dma((6,)),
            dma, dma,
            dma((3,)), dma((3, 2, half)),
            dma, dma,
            dma, dma((2, half + 1)),
            dma, dma((2, 2, 2)),
            dma, dma((2, 2, half - 2, 2)),
            dma, dma,
        ],
        compiler_params=pltpu.CompilerParams(
            collective_id=0, has_side_effects=True, vmem_limit_bytes=48 * 1024 * 1024
        ),
    )(
        step_size,
        *[pltpu.with_memory_space_constraint(x, pltpu.HBM) for x in (
            kept_blocks.reshape(-1),
            activations,
            cotangent.reshape(pairs, 2, rows, hid),
            weight,
            residual[0],
        )]
    )
    input_grad, residual_out, owned = pl.pallas_call(
        place,
        out_shape=tuple(jax.ShapeDtypeStruct(x.shape, x.dtype) for x in results),
        in_specs=[vmem] * 3,
        out_specs=(hbm, hbm, hbm),
        scratch_shapes=[dma((3,))],
    )(*[pltpu.with_memory_space_constraint(x, pltpu.VMEM) for x in results])
    return (
        input_grad,
        residual_out[None],
        owned.reshape(1, 1, 1, width // BLK, BLK, BLK),
    )


def solution(mesh):
    return jax.shard_map(
        body,
        mesh=mesh,
        in_specs=(
            P(("dp", "tensor"), "fsdp"),
            P("dp", "tensor"),
            P("fsdp", "tensor"),
            P("dp", "fsdp", "tensor"),
            P(),
            P("dp", "fsdp", "tensor", None),
        ),
        out_specs=(
            P(("dp", "tensor"), "fsdp"),
            P("dp", "fsdp", "tensor"),
            P("dp", "fsdp", "tensor", None, None, None),
        ),
        check_vma=False,
    )
```

```python
import contextlib

import jax
import jax.numpy as jnp
from jax import lax
from jax.experimental import pallas as pl
from jax.experimental.pallas import tpu as pltpu
from jax.sharding import PartitionSpec as P

BLK = 128
MESH = pl.DeviceIdType.MESH
NT = (((1,), (1,)), ((), ()))
F32 = jnp.float32
BF16 = jnp.bfloat16
AHEAD = 2
scope = lambda name: contextlib.nullcontext()


def kernel(
    step_ref, kept_hbm, acts_ref, cot_hbm, w_hbm, res_hbm,
    ig_ref, ro_ref, ow_ref,
    full, cot, w, res, own, yout, yin, early, ring16, ring, sent, dpin, kept_ref,
    local_sem, pair_send, pair_recv, ag_send, ag_recv, ya_send, ya_recv,
    yr_send, yr_recv, re_send, re_recv, rs_send, rs_recv, dp_send, dp_recv,
):
    planes = cot.shape[0]
    half = planes // 2
    rows = cot.shape[2]
    part = rows // 2
    hid = cot.shape[3]
    cols = full.shape[4]
    a = lax.axis_index("dp")
    f = lax.axis_index("fsdp")
    t = lax.axis_index("tensor")
    groups = lax.axis_size("dp")
    z = t // 2
    par = t % 2

    def plane(p):
        return lax.rem(p + 2 * planes, planes)

    pair = (a, f, z * 2 + 1 - par)
    sign = (1, -1)
    zdev = [(a, f, plane(z + v) * 2 + par) for v in sign]
    zpair = [(a, f, plane(z + v) * 2 + 1 - par) for v in sign]

    def dpdev(k):
        return (lax.rem(a + k, groups), f, t)

    def remote(src, dst, send, recv, dev):
        return pltpu.make_async_remote_copy(
            src_ref=src, dst_ref=dst, send_sem=send, recv_sem=recv, device_id=dev, device_id_type=MESH
        )

    def take(ref, sem):
        pltpu.make_async_copy(ref, ref, sem).wait()

    def loop(first, last, f):
        lax.fori_loop(first, last, lambda i, c: (f(i), c)[1], 0)

    barrier = pltpu.get_barrier_semaphore()
    others = zdev + zpair + [pair] + [dpdev(k) for k in range(1, groups)]
    for dev in others:
        pl.semaphore_signal(barrier, inc=1, device_id=dev, device_id_type=MESH)

    loads = [
        pltpu.make_async_copy(acts_ref.at[:, pl.ds(0, cols)], full.at[0, z, par], local_sem.at[0]),
        pltpu.make_async_copy(acts_ref.at[:, pl.ds(cols, cols)], full.at[1, z, par], local_sem.at[1]),
        pltpu.make_async_copy(cot_hbm, cot, local_sem.at[2]),
        pltpu.make_async_copy(w_hbm, w, local_sem.at[3]),
        pltpu.make_async_copy(res_hbm, res, local_sem.at[4]),
        pltpu.make_async_copy(kept_hbm, kept_ref, local_sem.at[5]),
    ]
    for load in loads:
        load.start()

    with scope("bar"):
        pl.semaphore_wait(barrier, len(others))

    chains = ((1, par), (0, par), (0, 1 - par))

    def shorter(h, d):
        return lax.rem(h + d, 2)

    def hops(h, d):
        return half if h == d else half - 1

    def gather_copy(c, d, s):
        h, q = chains[c]
        ref = full.at[h, plane(z - sign[d] * s), q]
        return remote(ref, ref, ag_send.at[c], ag_recv.at[c, d, s], zdev[d])

    def gather_first(c, d):
        h = chains[c][0]
        ref = full.at[h, z, par]
        return remote(ref, ref, ag_send.at[c], ag_recv.at[c, d, 0], zpair[d] if c == 2 else zdev[d])

    def gather_arrival(c, d, s):
        h, q = chains[c]
        take(full.at[h, plane(z - sign[d] * (s + 1)), q], ag_recv.at[c, d, s])

    def across_copy(p):
        ref = full.at[1, p, par]
        return remote(ref, ref, ya_send, ya_recv, pair)

    def gather_step(s):
        for c in range(3):
            for d in range(2):
                h = chains[c][0]

                def arrive():
                    gather_arrival(c, d, s)
                    if h == 1:
                        across_copy(plane(z - sign[d] * (s + 1))).start()

                if h == d:
                    arrive()
                else:
                    pl.when(s + 1 < half)(arrive)

                @pl.when(s + 1 < hops(h, d))
                def _():
                    gather_copy(c, d, s + 1).start()

    def exchange(r):
        h, k = r % 2, half - r // 2

        def send(p):
            remote(yout.at[p, h], yin.at[p, h], yr_send, yr_recv.at[h, k], pair).start()

        send(plane(z + k))

        @pl.when((k > 0) & (k < half))
        def _():
            send(plane(z - k))

    def exchanged(h, k, n):
        take(yin.at[pl.ds(0, n), 0], yr_recv.at[h, k])

    def early_step(s):
        for h in range(2):
            @pl.when(s == 0)
            def _():
                exchanged(h, half, 1)

            @pl.when(s == 1)
            def _():
                exchanged(h, half - 1, 2)

            for d in range(2):
                p = plane(z + sign[d] * (half - s))

                def pass_on():
                    total = own[p, h] + yin[p, h].astype(F32)
                    early[d, h, s] = total.astype(BF16)
                    remote(
                        early.at[d, h, s], ring16.at[d, h, s],
                        re_send, re_recv.at[d, h, s], zdev[d],
                    ).start()

                if h == d:
                    @pl.when(s == 1)
                    def _():
                        take(ring16.at[d, h, 0], re_recv.at[d, h, 0])
                        own[p, h] = own[p, h] + ring16[d, h, 0].astype(F32)

                    pass_on()
                else:
                    pl.when(s == 1)(pass_on)

    def ring_step(r):
        h, k = r % 2, half - r // 2
        exchanged(h, k, 2)
        for d in range(2):
            p = plane(z + sign[d] * k)

            @pl.when(k == half - 2)
            def _():
                take(ring16.at[d, h, 1], re_recv.at[d, h, 1])
                own[p, h] = own[p, h] + ring16[d, h, 1].astype(F32)

            for i in range(2):
                lines = pl.ds(i * part, part)

                @pl.when(k < half - 2)
                def _():
                    take(ring.at[d, h, k, lines], rs_recv.at[d, h, k, i])
                    own[p, h, lines] = own[p, h, lines] + ring[d, h, k, lines]

                own[p, h, lines] = own[p, h, lines] + yin[p, h, lines].astype(F32)
                remote(
                    own.at[p, h, lines], ring.at[d, h, k - 1, lines],
                    rs_send, rs_recv.at[d, h, k - 1, i], zdev[d],
                ).start()

    def planes_of(b):
        return [plane(z + half // 2 + half * b + i) for i in range(half)]

    def partial(b, parity):
        x = jnp.concatenate([cot[p, parity] for p in planes_of(b)], axis=0)
        return lax.dot_general(x, w[...], NT, preferred_element_type=F32)

    def theirs(b):
        y = partial(b, 1 - par).astype(BF16)
        for i, p in enumerate(planes_of(b)):
            for h in range(2):
                yout[p, h] = y[i * rows:(i + 1) * rows, h * cols:(h + 1) * cols]

    def ours(b):
        y = partial(b, par)
        for i, p in enumerate(planes_of(b)):
            for h in range(2):
                own[p, h] = y[i * rows:(i + 1) * rows, h * cols:(h + 1) * cols]

    def gradient(g):
        h = g // 2
        lanes = pl.ds(pl.multiple_of((g % 2) * 2 * BLK, 2 * BLK), 2 * BLK)
        lines = pl.ds(pl.multiple_of(g * 2 * BLK, 2 * BLK), 2 * BLK)
        step = step_ref[0]
        kept = [kept_ref[i] for i in range(kept_ref.shape[0])]
        x = full[h, :, :, :, lanes].reshape(planes * 2 * rows, 2 * BLK)
        y = cot[...].reshape(planes * 2 * rows, hid)
        grad = lax.dot_general(x, y, (((0,), (0,)), ((), ())), preferred_element_type=F32)
        rounded = (res[lines].astype(F32) + step * grad).astype(BF16)
        for i in range(2):
            for o in range(groups):
                number = (2 * g + i) * groups + o
                hit = kept[0] == number
                for other in kept[1:]:
                    hit = jnp.logical_or(hit, other == number)
                keep = jnp.where(hit, 1.0, 0.0)
                block = rounded[i * BLK:(i + 1) * BLK, o * BLK:(o + 1) * BLK].astype(F32)
                here = pl.ds(pl.multiple_of((2 * g + i) * BLK, BLK), BLK)
                ro_ref[here, o * BLK:(o + 1) * BLK] = (block * (1.0 - keep)).astype(BF16)
                sent[o, here] = (block * keep).astype(BF16)
        for k in range(1, groups):
            remote(
                sent.at[lax.rem(a + k, groups), lines], dpin.at[k - 1, lines], dp_send, dp_recv, dpdev(k)
            ).start()

    share = 4 - 2 * lax.rem(f, 2)

    def done(s):
        return 1 + (s * share + 9 - 2 * share) // 3

    with scope("ld0"):
        loads[0].wait()
        loads[1].wait()
    for c in range(3):
        for d in range(2):
            gather_first(c, d).start()
    pair_copy = remote(full.at[0, z, par], full.at[0, z, par], pair_send, pair_recv, pair)
    with scope("ld2"):
        loads[2].wait()
        loads[3].wait()
    with scope("theirs"):
        theirs(0)
    loop(0, done(0) + AHEAD, exchange)
    pair_copy.start()
    across_copy(z).start()
    with scope("ours"):
        theirs(1)
        ours(0)
        ours(1)

    def slot(s):
        loop(done(s) + AHEAD, done(s + 1) + AHEAD, exchange)

        with scope("ag"):
            gather_step(s)

        @pl.when(s < 2)
        def _():
            with scope("early"):
                early_step(s)

        @pl.when(s >= 2)
        def _():
            with scope("rs"):
                loop(done(s), done(s + 1), ring_step)

    loop(0, half, slot)
    last = done(half)
    loop(last + AHEAD, planes + 2, exchange)
    take(full.at[0, z, 1 - par], pair_recv)
    for load in loads[4:]:
        load.wait()

    def after(g):
        @pl.when(g > 0)
        def _():
            with scope("rs"):
                ring_step(last - 1 + g)

        @pl.when(g == 1)
        def _():
            with scope("across"):
                take(full.at[1, :, 1 - par], ya_recv)

        @pl.when(g < 3)
        def _():
            with scope("grad"):
                loop((3 * g + 1) // 2, g + 2, gradient)

    loop(0, planes - last + 1, after)

    with scope("rs_last"):
        for h in range(2):
            exchanged(h, 0, 1)
            for i in range(2):
                lines = pl.ds(i * part, part)
                total = own[z, h, lines] + yin[z, h, lines].astype(F32)
                for d in range(2):
                    take(ring.at[d, h, 0, lines], rs_recv.at[d, h, 0, i])
                    total = total + ring[d, h, 0, lines]
                ig_ref[lines, h * cols:(h + 1) * cols] = total.astype(BF16)

    with scope("dpsum"):
        take(dpin, dp_recv)
        total = sent[a].astype(F32)
        for k in range(1, groups):
            total = total + dpin[k - 1].astype(F32)
        ow_ref[...] = total

    with scope("drain"):
        pair_copy.wait_send()
        for c in range(3):
            take(full.at[0, pl.ds(0, planes - 1), 0], ag_send.at[c])
        take(full.at[0, :, 0], ya_send)
        take(yout, yr_send)
        take(yout.at[pl.ds(0, 3)], re_send)
        take(own.at[pl.ds(0, 2 * (half - 2))], rs_send)
        take(dpin, dp_send)


def place(ig_in, ro_in, ow_in, ig_out, ro_out, ow_out, sem):
    copies = [
        pltpu.make_async_copy(src, dst, sem.at[i])
        for i, (src, dst) in enumerate(((ro_in, ro_out), (ow_in, ow_out), (ig_in, ig_out)))
    ]
    for copy in copies:
        copy.start()
    for copy in copies:
        copy.wait()


def body(activations, cotangent, weight, residual, step_size, kept_blocks):
    rows, width = activations.shape
    hid = cotangent.shape[1]
    pairs = cotangent.shape[0] // (2 * rows)
    half = pairs // 2
    cols = width // 2
    groups = lax.axis_size("dp")
    vmem = pl.BlockSpec(memory_space=pltpu.VMEM)
    smem = pl.BlockSpec(memory_space=pltpu.SMEM)
    hbm = pl.BlockSpec(memory_space=pltpu.HBM)
    dma = pltpu.SemaphoreType.DMA
    results = pl.pallas_call(
        kernel,
        out_shape=(
            pltpu.VMEM((rows, width), BF16),
            pltpu.VMEM((width, hid), BF16),
            pltpu.VMEM((width, BLK), F32),
        ),
        in_specs=[smem] + [hbm] * 5,
        out_specs=(vmem, vmem, vmem),
        scratch_shapes=[
            pltpu.VMEM((2, pairs, 2, rows, cols), BF16),
            pltpu.VMEM((pairs, 2, rows, hid), BF16),
            pltpu.VMEM((width, hid), BF16),
            pltpu.VMEM((width, hid), BF16),
            pltpu.VMEM((pairs, 2, rows, cols), F32),
            pltpu.VMEM((pairs, 2, rows, cols), BF16),
            pltpu.VMEM((pairs, 2, rows, cols), BF16),
            pltpu.VMEM((2, 2, 2, rows, cols), BF16),
            pltpu.VMEM((2, 2, 2, rows, cols), BF16),
            pltpu.VMEM((2, 2, half - 2, rows, cols), F32),
            pltpu.VMEM((groups, width, BLK), BF16),
            pltpu.VMEM((groups - 1, width, BLK), BF16),
            pltpu.SMEM(kept_blocks.shape[-1:], jnp.int32),
            dma((6,)),
            dma, dma,
            dma((3,)), dma((3, 2, half)),
            dma, dma,
            dma, dma((2, half + 1)),
            dma, dma((2, 2, 2)),
            dma, dma((2, 2, half - 2, 2)),
            dma, dma,
        ],
        compiler_params=pltpu.CompilerParams(
            collective_id=0, has_side_effects=True, vmem_limit_bytes=48 * 1024 * 1024
        ),
    )(
        step_size,
        *[pltpu.with_memory_space_constraint(x, pltpu.HBM) for x in (
            kept_blocks.reshape(-1),
            activations,
            cotangent.reshape(pairs, 2, rows, hid),
            weight,
            residual[0],
        )]
    )
    input_grad, residual_out, owned = pl.pallas_call(
        place,
        out_shape=tuple(jax.ShapeDtypeStruct(x.shape, x.dtype) for x in results),
        in_specs=[vmem] * 3,
        out_specs=(hbm, hbm, hbm),
        scratch_shapes=[dma((3,))],
    )(*[pltpu.with_memory_space_constraint(x, pltpu.VMEM) for x in results])
    return (
        input_grad,
        residual_out[None],
        owned.reshape(1, 1, 1, width // BLK, BLK, BLK),
    )


def solution(mesh):
    return jax.shard_map(
        body,
        mesh=mesh,
        in_specs=(
            P(("dp", "tensor"), "fsdp"),
            P("dp", "tensor"),
            P("fsdp", "tensor"),
            P("dp", "fsdp", "tensor"),
            P(),
            P("dp", "fsdp", "tensor", None),
        ),
        out_specs=(
            P(("dp", "tensor"), "fsdp"),
            P("dp", "fsdp", "tensor"),
            P("dp", "fsdp", "tensor", None, None, None),
        ),
        check_vma=False,
    )
```

```python
import contextlib

import jax
import jax.numpy as jnp
from jax import lax
from jax.experimental import pallas as pl
from jax.experimental.pallas import tpu as pltpu
from jax.sharding import PartitionSpec as P

BLK = 128
MESH = pl.DeviceIdType.MESH
NT = (((1,), (1,)), ((), ()))
F32 = jnp.float32
BF16 = jnp.bfloat16
AHEAD = 2
scope = lambda name: contextlib.nullcontext()


def kernel(
    step_ref, kept_hbm, acts_ref, cot_hbm, w_hbm, res_hbm,
    ig_ref, ro_ref, ow_ref,
    full, cot, w, res, own, yout, yin, early, ring16, ring, sent, dpin, kept_ref,
    local_sem, pair_send, pair_recv, ag_send, ag_recv, ya_send, ya_recv,
    yr_send, yr_recv, re_send, re_recv, rs_send, rs_recv, dp_send, dp_recv,
):
    planes = cot.shape[0]
    half = planes // 2
    rows = cot.shape[2]
    part = rows // 2
    hid = cot.shape[3]
    cols = full.shape[4]
    a = lax.axis_index("dp")
    f = lax.axis_index("fsdp")
    t = lax.axis_index("tensor")
    groups = lax.axis_size("dp")
    z = t // 2
    par = t % 2

    def plane(p):
        return lax.rem(p + 2 * planes, planes)

    pair = (a, f, z * 2 + 1 - par)
    sign = (1, -1)
    zdev = [(a, f, plane(z + v) * 2 + par) for v in sign]
    zpair = [(a, f, plane(z + v) * 2 + 1 - par) for v in sign]

    def dpdev(k):
        return (lax.rem(a + k, groups), f, t)

    def remote(src, dst, send, recv, dev):
        return pltpu.make_async_remote_copy(
            src_ref=src, dst_ref=dst, send_sem=send, recv_sem=recv, device_id=dev, device_id_type=MESH
        )

    def take(ref, sem):
        pltpu.make_async_copy(ref, ref, sem).wait()

    def loop(first, last, f):
        lax.fori_loop(first, last, lambda i, c: (f(i), c)[1], 0)

    barrier = pltpu.get_barrier_semaphore()
    others = zdev + zpair + [pair] + [dpdev(k) for k in range(1, groups)]
    for dev in others:
        pl.semaphore_signal(barrier, inc=1, device_id=dev, device_id_type=MESH)

    loads = [
        pltpu.make_async_copy(acts_ref.at[:, pl.ds(0, cols)], full.at[0, z, par], local_sem.at[0]),
        pltpu.make_async_copy(acts_ref.at[:, pl.ds(cols, cols)], full.at[1, z, par], local_sem.at[1]),
        pltpu.make_async_copy(cot_hbm, cot, local_sem.at[2]),
        pltpu.make_async_copy(w_hbm, w, local_sem.at[3]),
        pltpu.make_async_copy(res_hbm, res, local_sem.at[4]),
        pltpu.make_async_copy(kept_hbm, kept_ref, local_sem.at[5]),
    ]
    for load in loads:
        load.start()

    with scope("bar"):
        pl.semaphore_wait(barrier, len(others))

    chains = ((1, par), (0, par), (0, 1 - par))

    def shorter(h, d):
        return lax.rem(h + d, 2)

    def hops(h, d):
        return half if h == d else half - 1

    def gather_copy(c, d, s):
        h, q = chains[c]
        ref = full.at[h, plane(z - sign[d] * s), q]
        return remote(ref, ref, ag_send.at[c], ag_recv.at[c, d, lax.rem(s, 3)], zdev[d])

    def gather_first(c, d):
        h = chains[c][0]
        ref = full.at[h, z, par]
        return remote(ref, ref, ag_send.at[c], ag_recv.at[c, d, 0], zpair[d] if c == 2 else zdev[d])

    def gather_arrival(c, d, s):
        h, q = chains[c]
        take(full.at[h, plane(z - sign[d] * (s + 1)), q], ag_recv.at[c, d, lax.rem(s, 3)])

    def across_copy(p):
        ref = full.at[1, p, par]
        return remote(ref, ref, ya_send, ya_recv, pair)

    def gather_step(s):
        for c in range(3):
            for d in range(2):
                h = chains[c][0]

                def arrive():
                    gather_arrival(c, d, s)
                    if h == 1:
                        across_copy(plane(z - sign[d] * (s + 1))).start()

                if h == d:
                    arrive()
                else:
                    pl.when(s + 1 < half)(arrive)

                @pl.when(s + 1 < hops(h, d))
                def _():
                    gather_copy(c, d, s + 1).start()

    def exchange(r):
        h, k = r % 2, half - r // 2

        def send(p):
            remote(yout.at[p, h], yin.at[p, h], yr_send, yr_recv.at[h, k], pair).start()

        send(plane(z + k))

        @pl.when((k > 0) & (k < half))
        def _():
            send(plane(z - k))

    def exchanged(h, k, n):
        take(yin.at[pl.ds(0, n), 0], yr_recv.at[h, k])

    def early_step(s):
        for h in range(2):
            @pl.when(s == 0)
            def _():
                exchanged(h, half, 1)

            @pl.when(s == 1)
            def _():
                exchanged(h, half - 1, 2)

            for d in range(2):
                p = plane(z + sign[d] * (half - s))

                def pass_on():
                    total = own[p, h] + yin[p, h].astype(F32)
                    early[d, h, s] = total.astype(BF16)
                    remote(
                        early.at[d, h, s], ring16.at[d, h, s],
                        re_send, re_recv.at[d, h, s], zdev[d],
                    ).start()

                if h == d:
                    @pl.when(s == 1)
                    def _():
                        take(ring16.at[d, h, 0], re_recv.at[d, h, 0])
                        own[p, h] = own[p, h] + ring16[d, h, 0].astype(F32)

                    pass_on()
                else:
                    pl.when(s == 1)(pass_on)

    def ring_step(r):
        h, k = r % 2, half - r // 2
        exchanged(h, k, 2)
        for d in range(2):
            p = plane(z + sign[d] * k)

            @pl.when(k == half - 2)
            def _():
                take(ring16.at[d, h, 1], re_recv.at[d, h, 1])
                own[p, h] = own[p, h] + ring16[d, h, 1].astype(F32)

            for i in range(2):
                lines = pl.ds(i * part, part)

                @pl.when(k < half - 2)
                def _():
                    take(ring.at[d, h, k, lines], rs_recv.at[d, h, lax.rem(k, 3), i])
                    own[p, h, lines] = own[p, h, lines] + ring[d, h, k, lines]

                own[p, h, lines] = own[p, h, lines] + yin[p, h, lines].astype(F32)
                remote(
                    own.at[p, h, lines], ring.at[d, h, k - 1, lines],
                    rs_send, rs_recv.at[d, h, lax.rem(k - 1, 3), i], zdev[d],
                ).start()

    def planes_of(b):
        return [plane(z + half // 2 + half * b + i) for i in range(half)]

    def partial(b, parity):
        x = jnp.concatenate([cot[p, parity] for p in planes_of(b)], axis=0)
        return lax.dot_general(x, w[...], NT, preferred_element_type=F32)

    def theirs(b):
        y = partial(b, 1 - par).astype(BF16)
        for i, p in enumerate(planes_of(b)):
            for h in range(2):
                yout[p, h] = y[i * rows:(i + 1) * rows, h * cols:(h + 1) * cols]

    def ours(b):
        y = partial(b, par)
        for i, p in enumerate(planes_of(b)):
            for h in range(2):
                own[p, h] = y[i * rows:(i + 1) * rows, h * cols:(h + 1) * cols]

    def gradient(g):
        h = g // 2
        lanes = pl.ds(pl.multiple_of((g % 2) * 2 * BLK, 2 * BLK), 2 * BLK)
        lines = pl.ds(pl.multiple_of(g * 2 * BLK, 2 * BLK), 2 * BLK)
        step = step_ref[0]
        kept = [kept_ref[i] for i in range(kept_ref.shape[0])]
        x = full[h, :, :, :, lanes].reshape(planes * 2 * rows, 2 * BLK)
        y = cot[...].reshape(planes * 2 * rows, hid)
        grad = lax.dot_general(x, y, (((0,), (0,)), ((), ())), preferred_element_type=F32)
        rounded = (res[lines].astype(F32) + step * grad).astype(BF16)
        for i in range(2):
            for o in range(groups):
                number = (2 * g + i) * groups + o
                hit = kept[0] == number
                for other in kept[1:]:
                    hit = jnp.logical_or(hit, other == number)
                keep = jnp.where(hit, 1.0, 0.0)
                block = rounded[i * BLK:(i + 1) * BLK, o * BLK:(o + 1) * BLK].astype(F32)
                here = pl.ds(pl.multiple_of((2 * g + i) * BLK, BLK), BLK)
                ro_ref[here, o * BLK:(o + 1) * BLK] = (block * (1.0 - keep)).astype(BF16)
                sent[o, here] = (block * keep).astype(BF16)
        for k in (2, 1, 3):
            remote(
                sent.at[lax.rem(a + k, groups), lines], dpin.at[k - 1, lines], dp_send, dp_recv, dpdev(k)
            ).start()

    share = 5 - 2 * lax.rem(f, 2)

    def done(s):
        return (s * share + 12 - 2 * share) // 3

    with scope("ld0"):
        loads[0].wait()
        loads[1].wait()
    for c in range(3):
        for d in range(2):
            gather_first(c, d).start()
    pair_copy = remote(full.at[0, z, par], full.at[0, z, par], pair_send, pair_recv, pair)
    with scope("ld2"):
        loads[2].wait()
        loads[3].wait()
    with scope("theirs"):
        theirs(0)
    loop(0, done(0) + AHEAD, exchange)
    pair_copy.start()
    across_copy(z).start()
    with scope("ours"):
        theirs(1)
        ours(0)
        ours(1)

    def slot(s):
        def exchange_next():
            loop(done(s) + AHEAD, done(s + 1) + AHEAD, exchange)

        pl.when(s < half - 1)(exchange_next)

        with scope("ag"):
            gather_step(s)

        pl.when(s == half - 1)(exchange_next)

        @pl.when(s == half - 1)
        def _():
            take(full.at[0, z, 1 - par], pair_recv)
            for load in loads[4:]:
                load.wait()
            with scope("grad"):
                loop(0, 2, gradient)

        @pl.when(s < 2)
        def _():
            with scope("early"):
                early_step(s)

        @pl.when(s >= 2)
        def _():
            with scope("rs"):
                loop(done(s), done(s + 1), ring_step)

    loop(0, half, slot)
    last = done(half)

    def after(r):
        @pl.when(r + AHEAD < planes + 2)
        def _():
            exchange(r + AHEAD)

        @pl.when(r == last + lax.rem(f, 2))
        def _():
            with scope("across"):
                take(full.at[1, :, 1 - par], ya_recv)
            with scope("grad"):
                loop(2, 4, gradient)

        with scope("rs"):
            ring_step(r)

    loop(last, planes, after)

    with scope("rs_last"):
        for h in range(2):
            exchanged(h, 0, 1)
            for i in range(2):
                lines = pl.ds(i * part, part)
                total = own[z, h, lines] + yin[z, h, lines].astype(F32)
                for d in range(2):
                    take(ring.at[d, h, 0, lines], rs_recv.at[d, h, 0, i])
                    total = total + ring[d, h, 0, lines]
                ig_ref[lines, h * cols:(h + 1) * cols] = total.astype(BF16)

    with scope("dpsum"):
        take(dpin, dp_recv)
        total = sent[a].astype(F32)
        for k in range(1, groups):
            total = total + dpin[k - 1].astype(F32)
        ow_ref[...] = total

    with scope("drain"):
        pair_copy.wait_send()
        for c in range(3):
            take(full.at[0, pl.ds(0, planes - 1), 0], ag_send.at[c])
        take(full.at[0, :, 0], ya_send)
        take(yout, yr_send)
        take(yout.at[pl.ds(0, 3)], re_send)
        take(own.at[pl.ds(0, 2 * (half - 2))], rs_send)
        take(dpin, dp_send)


def place(ig_in, ro_in, ow_in, ig_out, ro_out, ow_out, sem):
    copies = [
        pltpu.make_async_copy(src, dst, sem.at[i])
        for i, (src, dst) in enumerate(((ro_in, ro_out), (ow_in, ow_out), (ig_in, ig_out)))
    ]
    for copy in copies:
        copy.start()
    for copy in copies:
        copy.wait()


def body(activations, cotangent, weight, residual, step_size, kept_blocks):
    rows, width = activations.shape
    hid = cotangent.shape[1]
    pairs = cotangent.shape[0] // (2 * rows)
    half = pairs // 2
    cols = width // 2
    groups = lax.axis_size("dp")
    vmem = pl.BlockSpec(memory_space=pltpu.VMEM)
    smem = pl.BlockSpec(memory_space=pltpu.SMEM)
    hbm = pl.BlockSpec(memory_space=pltpu.HBM)
    dma = pltpu.SemaphoreType.DMA
    results = pl.pallas_call(
        kernel,
        out_shape=(
            pltpu.VMEM((rows, width), BF16),
            pltpu.VMEM((width, hid), BF16),
            pltpu.VMEM((width, BLK), F32),
        ),
        in_specs=[smem] + [hbm] * 5,
        out_specs=(vmem, vmem, vmem),
        scratch_shapes=[
            pltpu.VMEM((2, pairs, 2, rows, cols), BF16),
            pltpu.VMEM((pairs, 2, rows, hid), BF16),
            pltpu.VMEM((width, hid), BF16),
            pltpu.VMEM((width, hid), BF16),
            pltpu.VMEM((pairs, 2, rows, cols), F32),
            pltpu.VMEM((pairs, 2, rows, cols), BF16),
            pltpu.VMEM((pairs, 2, rows, cols), BF16),
            pltpu.VMEM((2, 2, 2, rows, cols), BF16),
            pltpu.VMEM((2, 2, 2, rows, cols), BF16),
            pltpu.VMEM((2, 2, half - 2, rows, cols), F32),
            pltpu.VMEM((groups, width, BLK), BF16),
            pltpu.VMEM((groups - 1, width, BLK), BF16),
            pltpu.SMEM(kept_blocks.shape[-1:], jnp.int32),
            dma((6,)),
            dma, dma,
            dma((3,)), dma((3, 2, 3)),
            dma, dma,
            dma, dma((2, half + 1)),
            dma, dma((2, 2, 2)),
            dma, dma((2, 2, 3, 2)),
            dma, dma,
        ],
        compiler_params=pltpu.CompilerParams(
            collective_id=0, has_side_effects=True, vmem_limit_bytes=48 * 1024 * 1024
        ),
    )(
        step_size,
        *[pltpu.with_memory_space_constraint(x, pltpu.HBM) for x in (
            kept_blocks.reshape(-1),
            activations,
            cotangent.reshape(pairs, 2, rows, hid),
            weight,
            residual[0],
        )]
    )
    input_grad, residual_out, owned = pl.pallas_call(
        place,
        out_shape=tuple(jax.ShapeDtypeStruct(x.shape, x.dtype) for x in results),
        in_specs=[vmem] * 3,
        out_specs=(hbm, hbm, hbm),
        scratch_shapes=[dma((3,))],
    )(*[pltpu.with_memory_space_constraint(x, pltpu.VMEM) for x in results])
    return (
        input_grad,
        residual_out[None],
        owned.reshape(1, 1, 1, width // BLK, BLK, BLK),
    )


def solution(mesh):
    return jax.shard_map(
        body,
        mesh=mesh,
        in_specs=(
            P(("dp", "tensor"), "fsdp"),
            P("dp", "tensor"),
            P("fsdp", "tensor"),
            P("dp", "fsdp", "tensor"),
            P(),
            P("dp", "fsdp", "tensor", None),
        ),
        out_specs=(
            P(("dp", "tensor"), "fsdp"),
            P("dp", "fsdp", "tensor"),
            P("dp", "fsdp", "tensor", None, None, None),
        ),
        check_vma=False,
    )
```

```python
import contextlib

import jax
import jax.numpy as jnp
from jax import lax
from jax.experimental import pallas as pl
from jax.experimental.pallas import tpu as pltpu
from jax.sharding import PartitionSpec as P

BLK = 128
MESH = pl.DeviceIdType.MESH
NT = (((1,), (1,)), ((), ()))
F32 = jnp.float32
BF16 = jnp.bfloat16
AHEAD = 2
scope = lambda name: contextlib.nullcontext()


def kernel(
    step_ref, kept_hbm, acts_ref, cot_hbm, w_hbm, res_hbm,
    ig_ref, ro_ref, ow_ref,
    full, cot, w, res, own, yout, yin, early, ring16, ring, sent, dpin, kept_ref,
    local_sem, pair_send, pair_recv, ag_send, ag_recv, ya_send, ya_recv,
    yr_send, yr_recv, re_send, re_recv, rs_send, rs_recv, dp_send, dp_recv,
):
    planes = cot.shape[0]
    half = planes // 2
    rows = cot.shape[2]
    part = rows // 2
    hid = cot.shape[3]
    cols = full.shape[4]
    a = lax.axis_index("dp")
    f = lax.axis_index("fsdp")
    t = lax.axis_index("tensor")
    groups = lax.axis_size("dp")
    z = t // 2
    par = t % 2

    def plane(p):
        return lax.rem(p + 2 * planes, planes)

    pair = (a, f, z * 2 + 1 - par)
    sign = (1, -1)
    zdev = [(a, f, plane(z + v) * 2 + par) for v in sign]
    zpair = [(a, f, plane(z + v) * 2 + 1 - par) for v in sign]

    def dpdev(k):
        return (lax.rem(a + k, groups), f, t)

    def remote(src, dst, send, recv, dev):
        return pltpu.make_async_remote_copy(
            src_ref=src, dst_ref=dst, send_sem=send, recv_sem=recv, device_id=dev, device_id_type=MESH
        )

    def take(ref, sem):
        pltpu.make_async_copy(ref, ref, sem).wait()

    def loop(first, last, f):
        lax.fori_loop(first, last, lambda i, c: (f(i), c)[1], 0)

    barrier = pltpu.get_barrier_semaphore()
    others = zdev + zpair + [pair] + [dpdev(k) for k in range(1, groups)]
    for dev in others:
        pl.semaphore_signal(barrier, inc=1, device_id=dev, device_id_type=MESH)

    loads = [
        pltpu.make_async_copy(acts_ref.at[:, pl.ds(0, cols)], full.at[0, z, par], local_sem.at[0]),
        pltpu.make_async_copy(acts_ref.at[:, pl.ds(cols, cols)], full.at[1, z, par], local_sem.at[1]),
        pltpu.make_async_copy(cot_hbm, cot, local_sem.at[2]),
        pltpu.make_async_copy(w_hbm, w, local_sem.at[3]),
        pltpu.make_async_copy(res_hbm, res, local_sem.at[4]),
        pltpu.make_async_copy(kept_hbm, kept_ref, local_sem.at[5]),
    ]
    for load in loads:
        load.start()

    with scope("bar"):
        pl.semaphore_wait(barrier, len(others))

    chains = ((1, par), (0, par), (0, 1 - par))

    def shorter(h, d):
        return lax.rem(h + d, 2)

    def hops(h, d):
        return half if h == d else half - 1

    def gather_copy(c, d, s):
        h, q = chains[c]
        ref = full.at[h, plane(z - sign[d] * s), q]
        return remote(ref, ref, ag_send.at[c], ag_recv.at[c, d, lax.rem(s, 3)], zdev[d])

    def gather_first(c, d):
        h = chains[c][0]
        ref = full.at[h, z, par]
        return remote(ref, ref, ag_send.at[c], ag_recv.at[c, d, 0], zpair[d] if c == 2 else zdev[d])

    def gather_arrival(c, d, s):
        h, q = chains[c]
        take(full.at[h, plane(z - sign[d] * (s + 1)), q], ag_recv.at[c, d, lax.rem(s, 3)])

    def across_copy(p):
        ref = full.at[1, p, par]
        return remote(ref, ref, ya_send, ya_recv, pair)

    def gather_step(s):
        for c in range(3):
            for d in range(2):
                h = chains[c][0]

                def arrive():
                    gather_arrival(c, d, s)
                    if h == 1:
                        across_copy(plane(z - sign[d] * (s + 1))).start()

                if h == d:
                    arrive()
                else:
                    pl.when(s + 1 < half)(arrive)

                @pl.when(s + 1 < hops(h, d))
                def _():
                    gather_copy(c, d, s + 1).start()

    def exchange(r):
        h, k = r % 2, half - r // 2

        def send(p):
            remote(yout.at[p, h], yin.at[p, h], yr_send, yr_recv.at[h, k], pair).start()

        send(plane(z + k))

        @pl.when((k > 0) & (k < half))
        def _():
            send(plane(z - k))

    def exchanged(h, k, n):
        take(yin.at[pl.ds(0, n), 0], yr_recv.at[h, k])

    def early_step(s):
        for h in range(2):
            @pl.when(s == 0)
            def _():
                exchanged(h, half, 1)

            @pl.when(s == 1)
            def _():
                exchanged(h, half - 1, 2)

            for d in range(2):
                p = plane(z + sign[d] * (half - s))

                def pass_on():
                    total = own[p, h] + yin[p, h].astype(F32)
                    early[d, h, s] = total.astype(BF16)
                    remote(
                        early.at[d, h, s], ring16.at[d, h, s],
                        re_send, re_recv.at[d, h, s], zdev[d],
                    ).start()

                if h == d:
                    @pl.when(s == 1)
                    def _():
                        take(ring16.at[d, h, 0], re_recv.at[d, h, 0])
                        own[p, h] = own[p, h] + ring16[d, h, 0].astype(F32)

                    pass_on()
                else:
                    pl.when(s == 1)(pass_on)

    def ring_step(r):
        h, k = r % 2, half - r // 2
        exchanged(h, k, 2)
        for d in range(2):
            p = plane(z + sign[d] * k)
            own[p, h] = own[p, h] + yin[p, h].astype(F32)

        @pl.when(k == half - 2)
        def _():
            for d in range(2):
                p = plane(z + sign[d] * k)
                take(ring16.at[d, h, 1], re_recv.at[d, h, 1])
                own[p, h] = own[p, h] + ring16[d, h, 1].astype(F32)

        for i in range(2):
            lines = pl.ds(i * part, part)
            for d in range(2):
                p = plane(z + sign[d] * k)

                @pl.when(k < half - 2)
                def _():
                    take(ring.at[d, h, k, lines], rs_recv.at[d, h, lax.rem(k, 3), i])
                    own[p, h, lines] = own[p, h, lines] + ring[d, h, k, lines]

                remote(
                    own.at[p, h, lines], ring.at[d, h, k - 1, lines],
                    rs_send, rs_recv.at[d, h, lax.rem(k - 1, 3), i], zdev[d],
                ).start()

    def planes_of(b):
        return [plane(z + half // 2 + half * b + i) for i in range(half)]

    def partial(b, parity):
        x = jnp.concatenate([cot[p, parity] for p in planes_of(b)], axis=0)
        return lax.dot_general(x, w[...], NT, preferred_element_type=F32)

    def theirs(b):
        y = partial(b, 1 - par).astype(BF16)
        for i, p in enumerate(planes_of(b)):
            for h in range(2):
                yout[p, h] = y[i * rows:(i + 1) * rows, h * cols:(h + 1) * cols]

    def ours(b):
        y = partial(b, par)
        for i, p in enumerate(planes_of(b)):
            for h in range(2):
                own[p, h] = y[i * rows:(i + 1) * rows, h * cols:(h + 1) * cols]

    def gradient(g):
        h = g // 2
        lanes = pl.ds(pl.multiple_of((g % 2) * 2 * BLK, 2 * BLK), 2 * BLK)
        lines = pl.ds(pl.multiple_of(g * 2 * BLK, 2 * BLK), 2 * BLK)
        step = step_ref[0]
        kept = [kept_ref[i] for i in range(kept_ref.shape[0])]
        x = full[h, :, :, :, lanes].reshape(planes * 2 * rows, 2 * BLK)
        y = cot[...].reshape(planes * 2 * rows, hid)
        grad = lax.dot_general(x, y, (((0,), (0,)), ((), ())), preferred_element_type=F32)
        rounded = (res[lines].astype(F32) + step * grad).astype(BF16)
        for i in range(2):
            for o in range(groups):
                number = (2 * g + i) * groups + o
                hit = kept[0] == number
                for other in kept[1:]:
                    hit = jnp.logical_or(hit, other == number)
                keep = jnp.where(hit, 1.0, 0.0)
                block = rounded[i * BLK:(i + 1) * BLK, o * BLK:(o + 1) * BLK].astype(F32)
                here = pl.ds(pl.multiple_of((2 * g + i) * BLK, BLK), BLK)
                ro_ref[here, o * BLK:(o + 1) * BLK] = (block * (1.0 - keep)).astype(BF16)
                sent[o, here] = (block * keep).astype(BF16)
        for k in (2, 1, 3):
            remote(
                sent.at[lax.rem(a + k, groups), lines], dpin.at[k - 1, lines], dp_send, dp_recv, dpdev(k)
            ).start()

    share = 5 - 2 * lax.rem(f, 2)

    def done(s):
        return (s * share + 12 - 2 * share) // 3

    with scope("ld0"):
        loads[0].wait()
        loads[1].wait()
    for c in range(3):
        for d in range(2):
            gather_first(c, d).start()
    pair_copy = remote(full.at[0, z, par], full.at[0, z, par], pair_send, pair_recv, pair)
    with scope("ld2"):
        loads[2].wait()
        loads[3].wait()
    with scope("theirs"):
        theirs(0)
    loop(0, done(0) + AHEAD, exchange)
    pair_copy.start()
    across_copy(z).start()
    with scope("ours"):
        theirs(1)
        ours(0)
        ours(1)

    def slot(s):
        def exchange_next():
            loop(done(s) + AHEAD, done(s + 1) + AHEAD, exchange)

        pl.when(s < half - 1)(exchange_next)

        with scope("ag"):
            gather_step(s)

        pl.when(s == half - 1)(exchange_next)

        @pl.when(s == half - 1)
        def _():
            take(full.at[0, z, 1 - par], pair_recv)
            for load in loads[4:]:
                load.wait()
            with scope("grad"):
                loop(0, 2, gradient)

        @pl.when(s < 2)
        def _():
            with scope("early"):
                early_step(s)

        @pl.when(s >= 2)
        def _():
            with scope("rs"):
                loop(done(s), done(s + 1), ring_step)

    loop(0, half, slot)
    last = done(half)

    def after(r):
        @pl.when(r + AHEAD < planes + 2)
        def _():
            exchange(r + AHEAD)

        @pl.when(r == last + lax.rem(f, 2))
        def _():
            with scope("across"):
                take(full.at[1, :, 1 - par], ya_recv)
            with scope("grad"):
                loop(2, 4, gradient)

        with scope("rs"):
            ring_step(r)

    loop(last, planes, after)

    with scope("rs_last"):
        for h in range(2):
            exchanged(h, 0, 1)
            for i in range(2):
                lines = pl.ds(i * part, part)
                total = own[z, h, lines] + yin[z, h, lines].astype(F32)
                for d in range(2):
                    take(ring.at[d, h, 0, lines], rs_recv.at[d, h, 0, i])
                    total = total + ring[d, h, 0, lines]
                ig_ref[lines, h * cols:(h + 1) * cols] = total.astype(BF16)

    with scope("dpsum"):
        take(dpin, dp_recv)
        total = sent[a].astype(F32)
        for k in range(1, groups):
            total = total + dpin[k - 1].astype(F32)
        ow_ref[...] = total

    with scope("drain"):
        pair_copy.wait_send()
        for c in range(3):
            take(full.at[0, pl.ds(0, planes - 1), 0], ag_send.at[c])
        take(full.at[0, :, 0], ya_send)
        take(yout, yr_send)
        take(yout.at[pl.ds(0, 3)], re_send)
        take(own.at[pl.ds(0, 2 * (half - 2))], rs_send)
        take(dpin, dp_send)


def place(ig_in, ro_in, ow_in, ig_out, ro_out, ow_out, sem):
    copies = [
        pltpu.make_async_copy(src, dst, sem.at[i])
        for i, (src, dst) in enumerate(((ro_in, ro_out), (ow_in, ow_out), (ig_in, ig_out)))
    ]
    for copy in copies:
        copy.start()
    for copy in copies:
        copy.wait()


def body(activations, cotangent, weight, residual, step_size, kept_blocks):
    rows, width = activations.shape
    hid = cotangent.shape[1]
    pairs = cotangent.shape[0] // (2 * rows)
    half = pairs // 2
    cols = width // 2
    groups = lax.axis_size("dp")
    vmem = pl.BlockSpec(memory_space=pltpu.VMEM)
    smem = pl.BlockSpec(memory_space=pltpu.SMEM)
    hbm = pl.BlockSpec(memory_space=pltpu.HBM)
    dma = pltpu.SemaphoreType.DMA
    results = pl.pallas_call(
        kernel,
        out_shape=(
            pltpu.VMEM((rows, width), BF16),
            pltpu.VMEM((width, hid), BF16),
            pltpu.VMEM((width, BLK), F32),
        ),
        in_specs=[smem] + [hbm] * 5,
        out_specs=(vmem, vmem, vmem),
        scratch_shapes=[
            pltpu.VMEM((2, pairs, 2, rows, cols), BF16),
            pltpu.VMEM((pairs, 2, rows, hid), BF16),
            pltpu.VMEM((width, hid), BF16),
            pltpu.VMEM((width, hid), BF16),
            pltpu.VMEM((pairs, 2, rows, cols), F32),
            pltpu.VMEM((pairs, 2, rows, cols), BF16),
            pltpu.VMEM((pairs, 2, rows, cols), BF16),
            pltpu.VMEM((2, 2, 2, rows, cols), BF16),
            pltpu.VMEM((2, 2, 2, rows, cols), BF16),
            pltpu.VMEM((2, 2, half - 2, rows, cols), F32),
            pltpu.VMEM((groups, width, BLK), BF16),
            pltpu.VMEM((groups - 1, width, BLK), BF16),
            pltpu.SMEM(kept_blocks.shape[-1:], jnp.int32),
            dma((6,)),
            dma, dma,
            dma((3,)), dma((3, 2, 3)),
            dma, dma,
            dma, dma((2, half + 1)),
            dma, dma((2, 2, 2)),
            dma, dma((2, 2, 3, 2)),
            dma, dma,
        ],
        compiler_params=pltpu.CompilerParams(
            collective_id=0, has_side_effects=True, vmem_limit_bytes=48 * 1024 * 1024
        ),
    )(
        step_size,
        *[pltpu.with_memory_space_constraint(x, pltpu.HBM) for x in (
            kept_blocks.reshape(-1),
            activations,
            cotangent.reshape(pairs, 2, rows, hid),
            weight,
            residual[0],
        )]
    )
    input_grad, residual_out, owned = pl.pallas_call(
        place,
        out_shape=tuple(jax.ShapeDtypeStruct(x.shape, x.dtype) for x in results),
        in_specs=[vmem] * 3,
        out_specs=(hbm, hbm, hbm),
        scratch_shapes=[dma((3,))],
    )(*[pltpu.with_memory_space_constraint(x, pltpu.VMEM) for x in results])
    return (
        input_grad,
        residual_out[None],
        owned.reshape(1, 1, 1, width // BLK, BLK, BLK),
    )


def solution(mesh):
    return jax.shard_map(
        body,
        mesh=mesh,
        in_specs=(
            P(("dp", "tensor"), "fsdp"),
            P("dp", "tensor"),
            P("fsdp", "tensor"),
            P("dp", "fsdp", "tensor"),
            P(),
            P("dp", "fsdp", "tensor", None),
        ),
        out_specs=(
            P(("dp", "tensor"), "fsdp"),
            P("dp", "fsdp", "tensor"),
            P("dp", "fsdp", "tensor", None, None, None),
        ),
        check_vma=False,
    )
```
